256 devices in a mesh: dp: 4 (over y), tensor: 4 (over x), context: 16 (over z, core).
Axes of the slice: x: 4, y: 4, z: 8, core: 2. Of those that a mesh axis runs over, the one named last changes fastest.
Arguments:
- queries: bfloat16 [98304, 4096], P(('dp', 'context'), 'tensor'), parts along dimension 0, may hold values from -1.796875 to 1.796875
- key_vectors: bfloat16 [98304, 4096], P(('dp', 'context'), 'tensor'), parts along dimension 0, may hold values from -1.796875 to 1.796875
- value_vectors: bfloat16 [98304, 4096], P(('dp', 'context'), 'tensor'), parts along dimension 0, may hold values from -42 to 42
- log_decay: float32 [32, 98304], P('tensor', ('dp', 'context')), parts along dimension 1, may hold values from -0.6 to 0, as said below
- out_gain: float32 [4096], P('tensor'), may hold values from 0.1 to 1.9
Outputs:
- attended: bfloat16 [98304, 4096], P(('dp', 'context'), 'tensor'), parts along dimension 0
The draws below stay inside these ranges and needn't reach their ends.
There are 4 independent parts, one for each index of `dp`. The reference program is written for one: setup_inputs(seed, part) draws one part's arguments, and reference() takes and returns one part's arrays. A program takes and returns all parts, laid end to end along the dimension named above; an argument that names none is the same for every part. Nothing has to cross between parts.
Inputs may be any that keep to these rules, and one draw needn't show every extreme that they name: `log_decay`: entries are negative.
All inputs are finite; a program needn't handle non-finite values.
Results may differ from the reference program's by a relative error of at most 0.0055.
Values sent between devices are 32-bit elements; how exact they have to be, the bound alone decides.
A program may use at most 128 MiB of HBM per device.

```python
import math
import jax
import jax.numpy as jnp
from jax import lax

HEAD_TOTAL = 32
HEAD_DIM = 128
BLK = 512
DOCUMENT_LENGTH = 24576


def draw_value_vectors(key, part):
    first, second, third = jax.random.split(key, 3)
    width = HEAD_TOTAL * HEAD_DIM
    base = jax.random.truncated_normal(first, -4.0, 4.0, (DOCUMENT_LENGTH, width), jnp.float32)
    column = jnp.exp(jax.random.uniform(second, (width,), jnp.float32, math.log(0.3), math.log(3.0)))
    rising = 3.0 ** (jnp.arange(width, dtype=jnp.float32) / width - 0.5)
    row_scale = jnp.exp(jax.random.uniform(third, (DOCUMENT_LENGTH, 1), jnp.float32, math.log(0.5), math.log(2.0)))
    return (base * column[None, :] * rising[None, :] * row_scale).astype(jnp.bfloat16)


def draw_log_decay(key, part):
    key_rows = jax.random.split(key, 6)
    order = jax.random.permutation(key_rows[0], HEAD_TOTAL)
    slow_count = HEAD_TOTAL // 2
    slow = order < slow_count
    slow_rate = jnp.exp(jax.random.uniform(key_rows[1], (HEAD_TOTAL,), jnp.float32, math.log(0.05), math.log(0.5))) / DOCUMENT_LENGTH
    fast_rate = 1.0 / jax.random.uniform(key_rows[2], (HEAD_TOTAL,), jnp.float32, 30.0, 50.0)
    base_rate = jnp.where(slow, slow_rate, fast_rate)
    jitter = jnp.exp(jax.random.uniform(key_rows[3], (HEAD_TOTAL, DOCUMENT_LENGTH), jnp.float32, math.log(0.5), math.log(2.0)))
    value_rows = -base_rate[:, None] * jitter
    spike_location = jax.random.randint(key_rows[4], (HEAD_TOTAL, 2), 0, DOCUMENT_LENGTH)
    spike_length = jnp.log(jax.random.uniform(key_rows[5], (HEAD_TOTAL, 2), jnp.float32, 0.6, 0.8))
    token_position = jnp.arange(DOCUMENT_LENGTH)[None, :]
    for item_count in range(2):
        value_rows = value_rows + jnp.where(token_position == spike_location[:, item_count:item_count + 1], spike_length[:, item_count:item_count + 1], 0.0)
    return value_rows


def shard_levels(stream_key, extent, cuts, low, top_value):
    factor_of = 1.0
    for axis_at, shards_of in cuts:
        steps = jax.random.uniform(jax.random.fold_in(jax.random.fold_in(stream_key, 6), axis_at), (shards_of,), jnp.float32, low / len(cuts), top_value / len(cuts))
        factor_of = factor_of * jnp.repeat(jnp.exp(steps), extent[axis_at] // shards_of).reshape((-1,) + (1,) * (len(extent) - 1 - axis_at))
    return factor_of


def scatter_about(key, extent, spread, bound, cuts=(), held_as=jnp.bfloat16):
    result = jax.random.normal(key, extent, jnp.float32) * spread
    if len(cuts) > 0:
        result = shard_levels(key, extent, cuts, -0.22, 0.18) * result
    return jnp.clip(result, min=-bound, max=bound).astype(held_as)


def setup_inputs(seed: int = 0, part: int = 0) -> dict:
    key_of = jax.random.split(jax.random.key(seed), 6)
    part_splits = jax.random.split(jax.random.fold_in(key_of[5], part), 6)
    queries = scatter_about(part_splits[0], (DOCUMENT_LENGTH, HEAD_TOTAL * HEAD_DIM), 0.3, 1.796875, ((0, 16), (1, 4)))
    key_vectors = scatter_about(part_splits[1], (DOCUMENT_LENGTH, HEAD_TOTAL * HEAD_DIM), 0.3, 1.796875, ((0, 16), (1, 4)))
    value_vectors = draw_value_vectors(jax.random.fold_in(jax.random.fold_in(key_of[5], part), 71), part)
    log_decay = draw_log_decay(jax.random.fold_in(jax.random.fold_in(key_of[5], part), 71), part)
    out_gain = jnp.clip(1.0 + 0.18 * jax.random.normal(key_of[4], (HEAD_TOTAL * HEAD_DIM,), jnp.float32), 0.1, 1.9)
    return dict(queries=queries, key_vectors=key_vectors, value_vectors=value_vectors, log_decay=log_decay, out_gain=out_gain)


def reference(queries, key_vectors, value_vectors, log_decay, out_gain):
    block_count = DOCUMENT_LENGTH // BLK
    query_blocks = queries.reshape(block_count, BLK, HEAD_TOTAL, HEAD_DIM)
    key_blocks = key_vectors.reshape(block_count, BLK, HEAD_TOTAL, HEAD_DIM)
    value_blocks = value_vectors.reshape(block_count, BLK, HEAD_TOTAL, HEAD_DIM)
    decay_blocks = log_decay.reshape(HEAD_TOTAL, block_count, BLK).transpose(1, 0, 2)
    lower = jnp.arange(BLK)[:, None] >= jnp.arange(BLK)[None, :]

    def advance(state, pieces):
        query_b, key_b, value_b, decay_b = pieces
        cum = jnp.cumsum(decay_b, axis=1)
        total = cum[:, -1]
        scores = jnp.einsum('thd,shd->hts', query_b.astype(jnp.float32), key_b.astype(jnp.float32))
        diff = cum[:, :, None] - cum[:, None, :]
        weights = jnp.where(lower[None], scores * jnp.exp(jnp.where(lower[None], diff, 0.0)), 0.0).astype(jnp.bfloat16)
        intra = jnp.einsum('hts,she->the', weights.astype(jnp.float32), value_b.astype(jnp.float32))
        entering = state.astype(jnp.bfloat16)
        inter = jnp.einsum('thd,hde->the', query_b.astype(jnp.float32), entering.astype(jnp.float32))
        inter = inter * jnp.exp(cum).T[:, :, None]
        scaled = (key_b.astype(jnp.float32) * jnp.exp(total[None, :] - cum.T)[:, :, None]).astype(jnp.bfloat16)
        new_state = jnp.exp(total)[:, None, None] * state + jnp.einsum('shd,she->hde', scaled.astype(jnp.float32), value_b.astype(jnp.float32))
        return (new_state, intra + inter)
    start_state = jnp.zeros((HEAD_TOTAL, HEAD_DIM, HEAD_DIM), jnp.float32)
    final_state, mixed = lax.scan(advance, start_state, (query_blocks, key_blocks, value_blocks, decay_blocks))
    mixed = mixed.reshape(DOCUMENT_LENGTH, HEAD_TOTAL * HEAD_DIM)
    mean_sq = lax.optimization_barrier(jnp.mean(mixed * mixed, axis=1, keepdims=True))
    return (mixed * lax.rsqrt(mean_sq + 1e-06) * out_gain[None, :]).astype(jnp.bfloat16)
```

```python
import functools

import jax
import jax.numpy as jnp
from jax import lax
from jax.experimental import pallas as pl
from jax.experimental.pallas import tpu as pltpu
from jax.sharding import PartitionSpec as P

MESH = pl.DeviceIdType.MESH
DIM = 128
CHUNK = 256
HALF = CHUNK // 2
GROUP = 8
FEATURES = 4096
EARLY_HEADS = 4
F32, BF16 = jnp.float32, jnp.bfloat16


def dot_nt(a, b):
    return lax.dot_general(a, b, (((1,), (1,)), ((), ())), preferred_element_type=F32)


def dot_nn(a, b):
    return jnp.dot(a, b, preferred_element_type=F32)


def attend_kernel(
    heads, positions, chips, tensors,
    q_hbm, k_hbm, v_hbm, decay_ref,
    mixed_ref, squares_ref,
    qb, kb, vb, cum_row, key_row, chunk_decay, chunk_offset, device_total, cum_col, local_in,
    state, recv_a, send_b, recv_b, send_c, recv_c, send_d, entering, send_e, recv_e,
    load_sem, a_send, a_recv, b_send, b_recv, c_send, c_recv, d_send, d_recv, e_send, e_recv,
):
    chunks = positions // CHUNK
    homes = heads // 2
    me = lax.axis_index("context")
    rank = lax.axis_index("tensor")
    chip = lax.div(me, 2)
    core = lax.rem(me, 2)
    first_home = core * homes
    first_other = (1 - core) * homes
    mate = chip * 2 + (1 - core)

    def load(which, source, target, h):
        return pltpu.make_async_copy(
            source.at[:, pl.ds(pl.multiple_of(h * DIM, DIM), DIM)], target.at[h], load_sem.at[which, h]
        )

    def order(i):
        return lax.rem(first_other + i, heads)

    @pl.loop(0, heads)
    def _(i):
        load(0, k_hbm, kb, order(i)).start()
        load(1, v_hbm, vb, order(i)).start()

    barrier = pltpu.get_barrier_semaphore()
    pl.semaphore_signal(barrier, inc=1, device_id={"context": mate}, device_id_type=MESH)
    for o in range(1, chips):
        there = lax.rem(chip + o, chips) * 2 + core
        pl.semaphore_signal(barrier, inc=1, device_id={"context": there}, device_id_type=MESH)
    for o in range(1, tensors):
        pl.semaphore_signal(
            barrier, inc=1, device_id={"tensor": lax.rem(rank + o, tensors)}, device_id_type=MESH
        )

    @pl.loop(0, heads)
    def _(h):
        load(2, q_hbm, qb, h).start()

    lane = lax.broadcasted_iota(jnp.int32, (heads, DIM), 1)

    def running(x):
        for shift in (1, 2, 4, 8, 16, 32, 64):
            x = x + jnp.where(lane >= shift, pltpu.roll(x, shift, 1), 0.0)
        return x

    before = jnp.zeros((heads, DIM), F32)
    for c in range(chunks):
        left = running(decay_ref[:, c * CHUNK : c * CHUNK + HALF])
        right = running(decay_ref[:, c * CHUNK + HALF : (c + 1) * CHUNK])
        right = right + jnp.broadcast_to(left[:, DIM - 1 :], (heads, DIM))
        total = jnp.broadcast_to(right[:, DIM - 1 :], (heads, DIM))
        cum_row[:, c * CHUNK : c * CHUNK + HALF] = left
        cum_row[:, c * CHUNK + HALF : (c + 1) * CHUNK] = right
        key_row[:, c * CHUNK : c * CHUNK + HALF] = jnp.exp(total - left)
        key_row[:, c * CHUNK + HALF : (c + 1) * CHUNK] = jnp.exp(total - right)
        chunk_decay[c] = jnp.exp(total)
        chunk_offset[c] = before
        before = before + total
    device_total[...] = before

    eye = jnp.where(
        lax.broadcasted_iota(jnp.int32, (DIM, DIM), 0) == lax.broadcasted_iota(jnp.int32, (DIM, DIM), 1), 1.0, 0.0
    ).astype(BF16)

    def device_state(h):
        load(0, k_hbm, kb, h).wait()
        load(1, v_hbm, vb, h).wait()
        held = None
        for c in range(chunks):
            rows = slice(c * CHUNK, (c + 1) * CHUNK)
            turned = dot_nt(eye, kb[h, rows, :])
            scaled = (turned * key_row[pl.ds(h, 1), rows]).astype(BF16)
            added = dot_nn(scaled, vb[h, rows, :])
            held = added if held is None else held * chunk_decay[c, pl.ds(h, 1), :] + added
            if c + 1 < chunks:
                local_in[h, c + 1] = held.astype(BF16)
        state[h, :DIM, :] = held
        state[h, DIM:, :] = jnp.broadcast_to(device_total[pl.ds(h, 1), :], (GROUP, DIM))

    def copy_a(i):
        return pltpu.make_async_remote_copy(
            src_ref=state.at[first_other + i],
            dst_ref=recv_a.at[i],
            send_sem=a_send.at[i],
            recv_sem=a_recv.at[i],
            device_id={"context": mate},
            device_id_type=MESH,
        )

    def copy_b(j):
        return pltpu.make_async_remote_copy(
            src_ref=send_b.at[j],
            dst_ref=recv_b.at[chip],
            send_sem=b_send.at[j],
            recv_sem=b_recv.at[chip],
            device_id={"context": j * 2 + core},
            device_id_type=MESH,
        )

    def arrival_b(s):
        return pltpu.make_async_remote_copy(
            src_ref=send_b.at[s],
            dst_ref=recv_b.at[s],
            send_sem=b_send.at[s],
            recv_sem=b_recv.at[s],
            device_id={"context": s * 2 + core},
            device_id_type=MESH,
        )

    def copy_c(j):
        return pltpu.make_async_remote_copy(
            src_ref=send_c.at[j],
            dst_ref=recv_c.at[chip],
            send_sem=c_send.at[j],
            recv_sem=c_recv.at[chip],
            device_id={"context": j * 2 + core},
            device_id_type=MESH,
        )

    def arrival_c(s):
        return pltpu.make_async_remote_copy(
            src_ref=send_c.at[s],
            dst_ref=recv_c.at[s],
            send_sem=c_send.at[s],
            recv_sem=c_recv.at[s],
            device_id={"context": s * 2 + core},
            device_id_type=MESH,
        )

    def copy_d(i):
        return pltpu.make_async_remote_copy(
            src_ref=send_d.at[i],
            dst_ref=entering.at[first_home + i],
            send_sem=d_send.at[i],
            recv_sem=d_recv.at[i],
            device_id={"context": mate},
            device_id_type=MESH,
        )

    def arrival_d(i):
        return pltpu.make_async_remote_copy(
            src_ref=send_d.at[i],
            dst_ref=entering.at[first_other + i],
            send_sem=d_send.at[i],
            recv_sem=d_recv.at[i],
            device_id={"context": mate},
            device_id_type=MESH,
        )

    def copy_e(half, o):
        return pltpu.make_async_remote_copy(
            src_ref=send_e.at[half],
            dst_ref=recv_e.at[half, rank],
            send_sem=e_send.at[half, o - 1],
            recv_sem=e_recv.at[half, rank],
            device_id={"tensor": lax.rem(rank + o, tensors)},
            device_id_type=MESH,
        )

    def arrival_e(half, o):
        there = lax.rem(rank + o, tensors)
        return pltpu.make_async_remote_copy(
            src_ref=send_e.at[half],
            dst_ref=recv_e.at[half, there],
            send_sem=e_send.at[half, o - 1],
            recv_sem=e_recv.at[half, there],
            device_id={"tensor": there},
            device_id_type=MESH,
        )

    part = DIM // 2
    device_state(first_other)
    pl.semaphore_wait(barrier, chips + tensors - 1)
    copy_a(0).start()

    @pl.loop(1, homes)
    def _(i):
        device_state(first_other + i)
        copy_a(i).start()

    def pair(i):
        own = state[first_home + i]
        came = recv_a[i]
        return jnp.where(core == 0, own, came), jnp.where(core == 0, came, own)

    @pl.loop(0, homes)
    def _(i):
        device_state(first_home + i)
        copy_a(i).wait_recv()
        earlier, later = pair(i)
        whole = jnp.exp(later[DIM : DIM + 1, :]) * earlier[:DIM, :] + later[:DIM, :]
        total = earlier[DIM:, :] + later[DIM:, :]
        for side in range(2):
            j = i * 2 + side
            send_b[j, :part, :] = whole[side * part : (side + 1) * part, :]
            send_b[j, part:, :] = total

            @pl.when(jnp.logical_and(j != chip, chip < chips - 1))
            def _():
                copy_b(j).start()

    lanes = lax.broadcasted_iota(jnp.int32, (GROUP, DIM), 1)

    @pl.loop(0, positions // DIM)
    def _(j):
        tile = cum_row[:, pl.ds(pl.multiple_of(j * DIM, DIM), DIM)]
        turned = jnp.concatenate([tile] * (DIM // heads), axis=0).T
        for h in range(heads):
            cum_col[h, pl.ds(pl.multiple_of(j * DIM, DIM), DIM), :] = jnp.broadcast_to(
                turned[:, h : h + 1], (DIM, DIM)
            )

    lower = lax.broadcasted_iota(jnp.int32, (DIM, DIM), 0) >= lax.broadcasted_iota(jnp.int32, (DIM, DIM), 1)

    def local(h):
        load(2, q_hbm, qb, h).wait()
        columns = pl.ds(pl.multiple_of(h * DIM, DIM), DIM)
        for c in range(chunks):
            rows = slice(c * CHUNK, (c + 1) * CHUNK)
            q, v = qb[h, rows, :], vb[h, rows, :]
            scores = dot_nt(q, kb[h, rows, :])
            at = cum_col[h, rows, :]
            by = cum_row[pl.ds(h, 1), rows]
            w00 = scores[:HALF, :HALF] * jnp.exp(jnp.where(lower, at[:HALF] - by[:, :HALF], -1e30))
            w10 = scores[HALF:, :HALF] * jnp.exp(at[HALF:] - by[:, :HALF])
            w11 = scores[HALF:, HALF:] * jnp.exp(jnp.where(lower, at[HALF:] - by[:, HALF:], -1e30))
            top = dot_nn(w00.astype(BF16), v[:HALF])
            bottom = dot_nn(jnp.concatenate([w10.astype(BF16), w11.astype(BF16)], axis=1), v)
            if c > 0:
                inter = dot_nn(q, local_in[h, c]) * jnp.exp(at)
                top = top + inter[:HALF]
                bottom = bottom + inter[HALF:]
            mixed_ref[c * CHUNK : c * CHUNK + HALF, columns] = top
            mixed_ref[c * CHUNK + HALF : (c + 1) * CHUNK, columns] = bottom

    @pl.loop(0, EARLY_HEADS)
    def _(h):
        local(h)

    prefix = jnp.zeros((part, DIM), F32)
    for s in range(chips - 1):

        @pl.when(chip == s)
        def _():
            recv_b[s] = send_b[s]

        @pl.when(chip != s)
        def _():
            arrival_b(s).wait_recv()

        prefix = prefix * jnp.exp(recv_b[s, part : part + 1, :]) + recv_b[s, :part, :]

        @pl.when(chip == s + 1)
        def _():
            recv_c[s + 1] = prefix

        @pl.when(chip != s + 1)
        def _():
            send_c[s + 1] = prefix
            copy_c(s + 1).start()

    @pl.loop(EARLY_HEADS, heads)
    def _(h):
        local(h)

    @pl.when(chip == 0)
    def _():
        recv_c[...] = jnp.zeros_like(recv_c)

    @pl.loop(0, homes)
    def _(i):
        for side in range(2):
            j = i * 2 + side

            @pl.when(jnp.logical_and(j != chip, chip > 0))
            def _():
                arrival_c(j).wait_recv()

        came = jnp.concatenate([recv_c[i * 2], recv_c[i * 2 + 1]], axis=0)
        earlier, _ = pair(i)
        after = jnp.exp(earlier[DIM : DIM + 1, :]) * came + earlier[:DIM, :]
        send_d[i] = jnp.where(core == 0, after, came)
        copy_d(i).start()
        entering[first_home + i] = jnp.where(core == 0, came, after)

    @pl.loop(0, homes)
    def _(i):
        arrival_d(i).wait_recv()

    tiles = chunks // 2
    groups = CHUNK // GROUP

    for half in range(2):

        def finish(r, found):
            c = half * tiles + r
            rows = pl.ds(pl.multiple_of(c * CHUNK, CHUNK), CHUNK)
            squares = None
            for h in range(heads):
                inter = dot_nn(qb[h, rows, :], entering[h].astype(BF16))
                gain = jnp.exp(cum_col[h, rows, :] + chunk_offset[c, pl.ds(h, 1), :])
                value = mixed_ref[rows, h * DIM : (h + 1) * DIM] + gain * inter
                mixed_ref[rows, h * DIM : (h + 1) * DIM] = value
                squares = value * value if squares is None else squares + value * value
            for g in range(groups):
                sums = jnp.sum(squares[g * GROUP : (g + 1) * GROUP, :], axis=1, keepdims=True)
                found = jnp.where(lanes == r * groups + g, sums, found)
            return found

        send_e[half] = lax.fori_loop(0, tiles, finish, jnp.zeros((GROUP, DIM), F32))
        for o in range(1, tensors):
            copy_e(half, o).start()

    for half in range(2):
        total = send_e[half]
        for o in range(1, tensors):
            arrival_e(half, o).wait_recv()
            total = total + recv_e[half, lax.rem(rank + o, tensors)]
        squares_ref[half] = total

    @pl.loop(0, homes)
    def _(i):
        copy_a(i).wait_send()
        copy_d(i).wait_send()

    @pl.loop(0, chips)
    def _(j):
        @pl.when(jnp.logical_and(j != chip, chip < chips - 1))
        def _():
            copy_b(j).wait_send()

        @pl.when(jnp.logical_and(j != chip, j > 0))
        def _():
            copy_c(j).wait_send()

    for half in range(2):
        for o in range(1, tensors):
            copy_e(half, o).wait_send()


def scale_kernel(mixed_ref, squares_ref, gain_ref, out_hbm, staged, sem):
    positions, width = mixed_ref.shape
    heads = width // DIM
    chunks = positions // CHUNK
    groups = CHUNK // GROUP

    def put(c):
        return pltpu.make_async_copy(staged.at[c], out_hbm.at[pl.ds(c * CHUNK, CHUNK), :], sem.at[c])

    for c in range(chunks):
        half, r = divmod(c, chunks // 2)
        scale = lax.rsqrt(squares_ref[half] / FEATURES + 1e-06)
        for g in range(0, groups, 2):
            rows = slice(c * CHUNK + g * GROUP, c * CHUNK + (g + 2) * GROUP)
            at = r * groups + g
            factor = jnp.concatenate(
                [
                    jnp.broadcast_to(scale[:, at : at + 1], (GROUP, DIM)),
                    jnp.broadcast_to(scale[:, at + 1 : at + 2], (GROUP, DIM)),
                ],
                axis=0,
            )
            for h in range(heads):
                cols = slice(h * DIM, (h + 1) * DIM)
                staged[c, g * GROUP : (g + 2) * GROUP, cols] = (
                    mixed_ref[rows, cols] * factor * gain_ref[:, cols]
                ).astype(BF16)
        put(c).start()
    for c in range(chunks):
        put(c).wait()


def shards(chips, tensors, queries, key_vectors, value_vectors, log_decay, out_gain):
    positions, width = queries.shape
    heads = width // DIM
    chunks = positions // CHUNK
    homes = heads // 2
    part = DIM // 2
    anywhere = pl.BlockSpec(memory_space=pl.ANY)
    vmem = pl.BlockSpec(memory_space=pltpu.VMEM)
    dma = pltpu.SemaphoreType.DMA
    mixed, squares = pl.pallas_call(
        functools.partial(attend_kernel, heads, positions, chips, tensors),
        out_shape=(
            jax.ShapeDtypeStruct((positions, width), F32),
            jax.ShapeDtypeStruct((2, GROUP, DIM), F32),
        ),
        in_specs=[anywhere, anywhere, anywhere, vmem],
        out_specs=(vmem, vmem),
        scratch_shapes=[
            pltpu.VMEM((heads, positions, DIM), BF16),
            pltpu.VMEM((heads, positions, DIM), BF16),
            pltpu.VMEM((heads, positions, DIM), BF16),
            pltpu.VMEM((heads, positions), F32),
            pltpu.VMEM((heads, positions), F32),
            pltpu.VMEM((chunks, heads, DIM), F32),
            pltpu.VMEM((chunks, heads, DIM), F32),
            pltpu.VMEM((heads, DIM), F32),
            pltpu.VMEM((heads, positions, DIM), F32),
            pltpu.VMEM((heads, chunks, DIM, DIM), BF16),
            pltpu.VMEM((heads, DIM + GROUP, DIM), F32),
            pltpu.VMEM((homes, DIM + GROUP, DIM), F32),
            pltpu.VMEM((chips, part + GROUP, DIM), F32),
            pltpu.VMEM((chips, part + GROUP, DIM), F32),
            pltpu.VMEM((chips, part, DIM), F32),
            pltpu.VMEM((chips, part, DIM), F32),
            pltpu.VMEM((homes, DIM, DIM), F32),
            pltpu.VMEM((heads, DIM, DIM), F32),
            pltpu.VMEM((2, GROUP, DIM), F32),
            pltpu.VMEM((2, tensors, GROUP, DIM), F32),
            dma((3, heads)),
            dma((homes,)),
            dma((homes,)),
            dma((chips,)),
            dma((chips,)),
            dma((chips,)),
            dma((chips,)),
            dma((homes,)),
            dma((homes,)),
            dma((2, tensors - 1)),
            dma((2, tensors)),
        ],
        compiler_params=pltpu.CompilerParams(
            collective_id=0, has_side_effects=True, vmem_limit_bytes=44 * 1024 * 1024
        ),
        name="attend",
    )(queries, key_vectors, value_vectors, log_decay)
    return pl.pallas_call(
        scale_kernel,
        out_shape=jax.ShapeDtypeStruct((positions, width), BF16),
        in_specs=[vmem, vmem, vmem],
        out_specs=anywhere,
        scratch_shapes=[pltpu.VMEM((chunks, CHUNK, width), BF16), dma((chunks,))],
        compiler_params=pltpu.CompilerParams(vmem_limit_bytes=16 * 1024 * 1024),
        name="scale",
    )(mixed, squares, out_gain.reshape(1, width))


def solution(mesh):
    chips, tensors = mesh.shape["context"] // 2, mesh.shape["tensor"]
    placed = (
        P(("dp", "context"), "tensor"),
        P(("dp", "context"), "tensor"),
        P(("dp", "context"), "tensor"),
        P("tensor", ("dp", "context")),
        P("tensor"),
    )
    return jax.shard_map(
        functools.partial(shards, chips, tensors),
        mesh=mesh,
        in_specs=placed,
        out_specs=P(("dp", "context"), "tensor"),
        check_vma=False,
    )
```

```python
import functools

import jax
import jax.numpy as jnp
from jax import lax
from jax.experimental import pallas as pl
from jax.experimental.pallas import tpu as pltpu
from jax.sharding import PartitionSpec as P

MESH = pl.DeviceIdType.MESH
DIM = 128
CHUNK = 256
HALF = CHUNK // 2
GROUP = 8
FEATURES = 4096
EARLY_HEADS = 4
F32, BF16 = jnp.float32, jnp.bfloat16


def dot_nt(a, b):
    return lax.dot_general(a, b, (((1,), (1,)), ((), ())), preferred_element_type=F32)


def dot_nn(a, b):
    return jnp.dot(a, b, preferred_element_type=F32)


def attend_kernel(
    heads, positions, chips, tensors,
    q_hbm, k_hbm, v_hbm, decay_hbm,
    mixed_ref, squares_ref,
    decay_ref, qb, kb, vb, cum_row, key_row, chunk_decay, chunk_offset, device_total, cum_col, local_in,
    state, recv_a, send_b, recv_b, send_c, recv_c, send_d, entering, send_e, recv_e,
    decay_sem, load_sem, a_send, a_recv, b_send, b_recv, c_send, c_recv, d_send, d_recv, e_send, e_recv,
):
    chunks = positions // CHUNK
    homes = heads // 2
    me = lax.axis_index("context")
    rank = lax.axis_index("tensor")
    chip = lax.div(me, 2)
    core = lax.rem(me, 2)
    first_home = core * homes
    first_other = (1 - core) * homes
    mate = chip * 2 + (1 - core)

    def load(which, source, target, h):
        return pltpu.make_async_copy(
            source.at[:, pl.ds(pl.multiple_of(h * DIM, DIM), DIM)], target.at[h], load_sem.at[which, h]
        )

    def order(i):
        return lax.rem(first_other + i, heads)

    decay_load = pltpu.make_async_copy(decay_hbm, decay_ref, decay_sem)
    decay_load.start()

    @pl.loop(0, heads)
    def _(i):
        load(0, k_hbm, kb, order(i)).start()
        load(1, v_hbm, vb, order(i)).start()

    barrier = pltpu.get_barrier_semaphore()
    pl.semaphore_signal(barrier, inc=1, device_id={"context": mate}, device_id_type=MESH)
    for o in range(1, chips):
        there = lax.rem(chip + o, chips) * 2 + core
        pl.semaphore_signal(barrier, inc=1, device_id={"context": there}, device_id_type=MESH)
    for o in range(1, tensors):
        pl.semaphore_signal(
            barrier, inc=1, device_id={"tensor": lax.rem(rank + o, tensors)}, device_id_type=MESH
        )

    @pl.loop(0, heads)
    def _(h):
        load(2, q_hbm, qb, h).start()

    lane = lax.broadcasted_iota(jnp.int32, (heads, DIM), 1)

    def running(x):
        for shift in (1, 2, 4, 8, 16, 32, 64):
            x = x + jnp.where(lane >= shift, pltpu.roll(x, shift, 1), 0.0)
        return x

    decay_load.wait()
    before = jnp.zeros((heads, DIM), F32)
    for c in range(chunks):
        left = running(decay_ref[:, c * CHUNK : c * CHUNK + HALF])
        right = running(decay_ref[:, c * CHUNK + HALF : (c + 1) * CHUNK])
        right = right + jnp.broadcast_to(left[:, DIM - 1 :], (heads, DIM))
        total = jnp.broadcast_to(right[:, DIM - 1 :], (heads, DIM))
        cum_row[:, c * CHUNK : c * CHUNK + HALF] = left
        cum_row[:, c * CHUNK + HALF : (c + 1) * CHUNK] = right
        key_row[:, c * CHUNK : c * CHUNK + HALF] = jnp.exp(total - left)
        key_row[:, c * CHUNK + HALF : (c + 1) * CHUNK] = jnp.exp(total - right)
        chunk_decay[c] = jnp.exp(total)
        chunk_offset[c] = before
        before = before + total
    device_total[...] = before

    eye = jnp.where(
        lax.broadcasted_iota(jnp.int32, (DIM, DIM), 0) == lax.broadcasted_iota(jnp.int32, (DIM, DIM), 1), 1.0, 0.0
    ).astype(BF16)

    def device_state(h):
        load(0, k_hbm, kb, h).wait()
        load(1, v_hbm, vb, h).wait()
        held = None
        for c in range(chunks):
            rows = slice(c * CHUNK, (c + 1) * CHUNK)
            turned = dot_nt(eye, kb[h, rows, :])
            scaled = (turned * key_row[pl.ds(h, 1), rows]).astype(BF16)
            added = dot_nn(scaled, vb[h, rows, :])
            held = added if held is None else held * chunk_decay[c, pl.ds(h, 1), :] + added
            if c + 1 < chunks:
                local_in[h, c + 1] = held.astype(BF16)
        state[h, :DIM, :] = held
        state[h, DIM:, :] = jnp.broadcast_to(device_total[pl.ds(h, 1), :], (GROUP, DIM))

    def copy_a(i):
        return pltpu.make_async_remote_copy(
            src_ref=state.at[first_other + i],
            dst_ref=recv_a.at[i],
            send_sem=a_send.at[i],
            recv_sem=a_recv.at[i],
            device_id={"context": mate},
            device_id_type=MESH,
        )

    def copy_b(j):
        return pltpu.make_async_remote_copy(
            src_ref=send_b.at[j],
            dst_ref=recv_b.at[chip],
            send_sem=b_send.at[j],
            recv_sem=b_recv.at[chip],
            device_id={"context": j * 2 + core},
            device_id_type=MESH,
        )

    def arrival_b(s):
        return pltpu.make_async_remote_copy(
            src_ref=send_b.at[s],
            dst_ref=recv_b.at[s],
            send_sem=b_send.at[s],
            recv_sem=b_recv.at[s],
            device_id={"context": s * 2 + core},
            device_id_type=MESH,
        )

    def copy_c(j):
        return pltpu.make_async_remote_copy(
            src_ref=send_c.at[j],
            dst_ref=recv_c.at[chip],
            send_sem=c_send.at[j],
            recv_sem=c_recv.at[chip],
            device_id={"context": j * 2 + core},
            device_id_type=MESH,
        )

    def arrival_c(s):
        return pltpu.make_async_remote_copy(
            src_ref=send_c.at[s],
            dst_ref=recv_c.at[s],
            send_sem=c_send.at[s],
            recv_sem=c_recv.at[s],
            device_id={"context": s * 2 + core},
            device_id_type=MESH,
        )

    def copy_d(i):
        return pltpu.make_async_remote_copy(
            src_ref=send_d.at[i],
            dst_ref=entering.at[first_home + i],
            send_sem=d_send.at[i],
            recv_sem=d_recv.at[i],
            device_id={"context": mate},
            device_id_type=MESH,
        )

    def arrival_d(i):
        return pltpu.make_async_remote_copy(
            src_ref=send_d.at[i],
            dst_ref=entering.at[first_other + i],
            send_sem=d_send.at[i],
            recv_sem=d_recv.at[i],
            device_id={"context": mate},
            device_id_type=MESH,
        )

    def copy_e(half, o):
        return pltpu.make_async_remote_copy(
            src_ref=send_e.at[half],
            dst_ref=recv_e.at[half, rank],
            send_sem=e_send.at[half, o - 1],
            recv_sem=e_recv.at[half, rank],
            device_id={"tensor": lax.rem(rank + o, tensors)},
            device_id_type=MESH,
        )

    def arrival_e(half, o):
        there = lax.rem(rank + o, tensors)
        return pltpu.make_async_remote_copy(
            src_ref=send_e.at[half],
            dst_ref=recv_e.at[half, there],
            send_sem=e_send.at[half, o - 1],
            recv_sem=e_recv.at[half, there],
            device_id={"tensor": there},
            device_id_type=MESH,
        )

    part = DIM // 2
    device_state(first_other)
    pl.semaphore_wait(barrier, chips + tensors - 1)
    copy_a(0).start()

    @pl.loop(1, homes)
    def _(i):
        device_state(first_other + i)
        copy_a(i).start()

    def pair(i):
        own = state[first_home + i]
        came = recv_a[i]
        return jnp.where(core == 0, own, came), jnp.where(core == 0, came, own)

    @pl.loop(0, homes)
    def _(i):
        device_state(first_home + i)
        copy_a(i).wait_recv()
        earlier, later = pair(i)
        whole = jnp.exp(later[DIM : DIM + 1, :]) * earlier[:DIM, :] + later[:DIM, :]
        total = earlier[DIM:, :] + later[DIM:, :]
        for side in range(2):
            j = i * 2 + side
            send_b[j, :part, :] = whole[side * part : (side + 1) * part, :]
            send_b[j, part:, :] = total

            @pl.when(jnp.logical_and(j != chip, chip < chips - 1))
            def _():
                copy_b(j).start()

    lanes = lax.broadcasted_iota(jnp.int32, (GROUP, DIM), 1)

    @pl.loop(0, positions // DIM)
    def _(j):
        tile = cum_row[:, pl.ds(pl.multiple_of(j * DIM, DIM), DIM)]
        turned = jnp.concatenate([tile] * (DIM // heads), axis=0).T
        for h in range(heads):
            cum_col[h, pl.ds(pl.multiple_of(j * DIM, DIM), DIM), :] = jnp.broadcast_to(
                turned[:, h : h + 1], (DIM, DIM)
            )

    lower = lax.broadcasted_iota(jnp.int32, (DIM, DIM), 0) >= lax.broadcasted_iota(jnp.int32, (DIM, DIM), 1)

    def local(h):
        load(2, q_hbm, qb, h).wait()
        columns = pl.ds(pl.multiple_of(h * DIM, DIM), DIM)
        for c in range(chunks):
            rows = slice(c * CHUNK, (c + 1) * CHUNK)
            q, v = qb[h, rows, :], vb[h, rows, :]
            scores = dot_nt(q, kb[h, rows, :])
            at = cum_col[h, rows, :]
            by = cum_row[pl.ds(h, 1), rows]
            w00 = scores[:HALF, :HALF] * jnp.exp(jnp.where(lower, at[:HALF] - by[:, :HALF], -1e30))
            w10 = scores[HALF:, :HALF] * jnp.exp(at[HALF:] - by[:, :HALF])
            w11 = scores[HALF:, HALF:] * jnp.exp(jnp.where(lower, at[HALF:] - by[:, HALF:], -1e30))
            top = dot_nn(w00.astype(BF16), v[:HALF])
            bottom = dot_nn(jnp.concatenate([w10.astype(BF16), w11.astype(BF16)], axis=1), v)
            if c > 0:
                inter = dot_nn(q, local_in[h, c]) * jnp.exp(at)
                top = top + inter[:HALF]
                bottom = bottom + inter[HALF:]
            mixed_ref[c * CHUNK : c * CHUNK + HALF, columns] = top
            mixed_ref[c * CHUNK + HALF : (c + 1) * CHUNK, columns] = bottom

    @pl.loop(0, EARLY_HEADS)
    def _(h):
        local(h)

    prefix = jnp.zeros((part, DIM), F32)
    for s in range(chips - 1):

        @pl.when(chip == s)
        def _():
            recv_b[s] = send_b[s]

        @pl.when(chip != s)
        def _():
            arrival_b(s).wait_recv()

        prefix = prefix * jnp.exp(recv_b[s, part : part + 1, :]) + recv_b[s, :part, :]

        @pl.when(chip == s + 1)
        def _():
            recv_c[s + 1] = prefix

        @pl.when(chip != s + 1)
        def _():
            send_c[s + 1] = prefix
            copy_c(s + 1).start()

    @pl.loop(EARLY_HEADS, heads)
    def _(h):
        local(h)

    @pl.when(chip == 0)
    def _():
        recv_c[...] = jnp.zeros_like(recv_c)

    @pl.loop(0, homes)
    def _(i):
        for side in range(2):
            j = i * 2 + side

            @pl.when(jnp.logical_and(j != chip, chip > 0))
            def _():
                arrival_c(j).wait_recv()

        came = jnp.concatenate([recv_c[i * 2], recv_c[i * 2 + 1]], axis=0)
        earlier, _ = pair(i)
        after = jnp.exp(earlier[DIM : DIM + 1, :]) * came + earlier[:DIM, :]
        send_d[i] = jnp.where(core == 0, after, came)
        copy_d(i).start()
        entering[first_home + i] = jnp.where(core == 0, came, after)

    @pl.loop(0, homes)
    def _(i):
        arrival_d(i).wait_recv()

    tiles = chunks // 2
    groups = CHUNK // GROUP

    for half in range(2):

        def finish(r, found):
            c = half * tiles + r
            rows = pl.ds(pl.multiple_of(c * CHUNK, CHUNK), CHUNK)
            squares = None
            for h in range(heads):
                inter = dot_nn(qb[h, rows, :], entering[h].astype(BF16))
                gain = jnp.exp(cum_col[h, rows, :] + chunk_offset[c, pl.ds(h, 1), :])
                value = mixed_ref[rows, h * DIM : (h + 1) * DIM] + gain * inter
                mixed_ref[rows, h * DIM : (h + 1) * DIM] = value
                squares = value * value if squares is None else squares + value * value
            for g in range(groups):
                sums = jnp.sum(squares[g * GROUP : (g + 1) * GROUP, :], axis=1, keepdims=True)
                found = jnp.where(lanes == r * groups + g, sums, found)
            return found

        send_e[half] = lax.fori_loop(0, tiles, finish, jnp.zeros((GROUP, DIM), F32))
        for o in range(1, tensors):
            copy_e(half, o).start()

    for half in range(2):
        total = send_e[half]
        for o in range(1, tensors):
            arrival_e(half, o).wait_recv()
            total = total + recv_e[half, lax.rem(rank + o, tensors)]
        squares_ref[half] = total

    @pl.loop(0, homes)
    def _(i):
        copy_a(i).wait_send()
        copy_d(i).wait_send()

    @pl.loop(0, chips)
    def _(j):
        @pl.when(jnp.logical_and(j != chip, chip < chips - 1))
        def _():
            copy_b(j).wait_send()

        @pl.when(jnp.logical_and(j != chip, j > 0))
        def _():
            copy_c(j).wait_send()

    for half in range(2):
        for o in range(1, tensors):
            copy_e(half, o).wait_send()


def scale_kernel(mixed_ref, squares_ref, gain_ref, out_hbm, staged, sem):
    positions, width = mixed_ref.shape
    heads = width // DIM
    chunks = positions // CHUNK
    groups = CHUNK // GROUP

    def put(c):
        return pltpu.make_async_copy(staged.at[c], out_hbm.at[pl.ds(c * CHUNK, CHUNK), :], sem.at[c])

    for c in range(chunks):
        half, r = divmod(c, chunks // 2)
        scale = lax.rsqrt(squares_ref[half] / FEATURES + 1e-06)
        for g in range(0, groups, 2):
            rows = slice(c * CHUNK + g * GROUP, c * CHUNK + (g + 2) * GROUP)
            at = r * groups + g
            factor = jnp.concatenate(
                [
                    jnp.broadcast_to(scale[:, at : at + 1], (GROUP, DIM)),
                    jnp.broadcast_to(scale[:, at + 1 : at + 2], (GROUP, DIM)),
                ],
                axis=0,
            )
            for h in range(heads):
                cols = slice(h * DIM, (h + 1) * DIM)
                staged[c, g * GROUP : (g + 2) * GROUP, cols] = (
                    mixed_ref[rows, cols] * factor * gain_ref[:, cols]
                ).astype(BF16)
        put(c).start()
    for c in range(chunks):
        put(c).wait()


def shards(chips, tensors, queries, key_vectors, value_vectors, log_decay, out_gain):
    positions, width = queries.shape
    heads = width // DIM
    chunks = positions // CHUNK
    homes = heads // 2
    part = DIM // 2
    anywhere = pl.BlockSpec(memory_space=pltpu.HBM)
    vmem = pl.BlockSpec(memory_space=pltpu.VMEM)
    dma = pltpu.SemaphoreType.DMA
    mixed, squares = pl.pallas_call(
        functools.partial(attend_kernel, heads, positions, chips, tensors),
        out_shape=(
            jax.ShapeDtypeStruct((positions, width), F32),
            jax.ShapeDtypeStruct((2, GROUP, DIM), F32),
        ),
        in_specs=[anywhere] * 4,
        out_specs=(vmem, vmem),
        scratch_shapes=[
            pltpu.VMEM((heads, positions), F32),
            pltpu.VMEM((heads, positions, DIM), BF16),
            pltpu.VMEM((heads, positions, DIM), BF16),
            pltpu.VMEM((heads, positions, DIM), BF16),
            pltpu.VMEM((heads, positions), F32),
            pltpu.VMEM((heads, positions), F32),
            pltpu.VMEM((chunks, heads, DIM), F32),
            pltpu.VMEM((chunks, heads, DIM), F32),
            pltpu.VMEM((heads, DIM), F32),
            pltpu.VMEM((heads, positions, DIM), F32),
            pltpu.VMEM((heads, chunks, DIM, DIM), BF16),
            pltpu.VMEM((heads, DIM + GROUP, DIM), F32),
            pltpu.VMEM((homes, DIM + GROUP, DIM), F32),
            pltpu.VMEM((chips, part + GROUP, DIM), F32),
            pltpu.VMEM((chips, part + GROUP, DIM), F32),
            pltpu.VMEM((chips, part, DIM), F32),
            pltpu.VMEM((chips, part, DIM), F32),
            pltpu.VMEM((homes, DIM, DIM), F32),
            pltpu.VMEM((heads, DIM, DIM), F32),
            pltpu.VMEM((2, GROUP, DIM), F32),
            pltpu.VMEM((2, tensors, GROUP, DIM), F32),
            dma,
            dma((3, heads)),
            dma((homes,)),
            dma((homes,)),
            dma((chips,)),
            dma((chips,)),
            dma((chips,)),
            dma((chips,)),
            dma((homes,)),
            dma((homes,)),
            dma((2, tensors - 1)),
            dma((2, tensors)),
        ],
        compiler_params=pltpu.CompilerParams(
            collective_id=0, has_side_effects=True, vmem_limit_bytes=32 * 1024 * 1024
        ),
        name="attend",
    )(*(pltpu.with_memory_space_constraint(x, pltpu.HBM) for x in (queries, key_vectors, value_vectors, log_decay)))
    return pl.pallas_call(
        scale_kernel,
        out_shape=jax.ShapeDtypeStruct((positions, width), BF16),
        in_specs=[vmem, vmem, vmem],
        out_specs=anywhere,
        scratch_shapes=[pltpu.VMEM((chunks, CHUNK, width), BF16), dma((chunks,))],
        compiler_params=pltpu.CompilerParams(vmem_limit_bytes=16 * 1024 * 1024),
        name="scale",
    )(mixed, squares, out_gain.reshape(1, width))


def solution(mesh):
    chips, tensors = mesh.shape["context"] // 2, mesh.shape["tensor"]
    placed = (
        P(("dp", "context"), "tensor"),
        P(("dp", "context"), "tensor"),
        P(("dp", "context"), "tensor"),
        P("tensor", ("dp", "context")),
        P("tensor"),
    )
    return jax.shard_map(
        functools.partial(shards, chips, tensors),
        mesh=mesh,
        in_specs=placed,
        out_specs=P(("dp", "context"), "tensor"),
        check_vma=False,
    )
```

```python
import functools

import jax
import jax.numpy as jnp
from jax import lax
from jax.experimental import pallas as pl
from jax.experimental.pallas import tpu as pltpu
from jax.sharding import PartitionSpec as P

MESH = pl.DeviceIdType.MESH
DIM = 128
CHUNK = 256
HALF = CHUNK // 2
GROUP = 8
FEATURES = 4096
EARLY_HEADS = 4
F32, BF16 = jnp.float32, jnp.bfloat16


def dot_nt(a, b):
    return lax.dot_general(a, b, (((1,), (1,)), ((), ())), preferred_element_type=F32)


def dot_nn(a, b):
    return jnp.dot(a, b, preferred_element_type=F32)


def attend_kernel(
    heads, positions, chips, tensors,
    q_hbm, k_hbm, v_hbm, decay_hbm,
    mixed_ref, squares_ref,
    decay_ref, qb, kb, vb, cum_row, key_row, chunk_decay, chunk_offset, device_total, cum_col, local_in,
    state, recv_a, send_b, recv_b, send_c, recv_c, send_d, entering, send_e, recv_e,
    decay_sem, load_sem, a_send, a_recv, b_send, b_recv, c_send, c_recv, d_send, d_recv, e_send, e_recv,
):
    chunks = positions // CHUNK
    homes = heads // 2
    me = lax.axis_index("context")
    rank = lax.axis_index("tensor")
    chip = lax.div(me, 2)
    core = lax.rem(me, 2)
    first_home = core * homes
    first_other = (1 - core) * homes
    mate = chip * 2 + (1 - core)

    def load(which, source, target, h):
        return pltpu.make_async_copy(
            source.at[:, pl.ds(pl.multiple_of(h * DIM, DIM), DIM)], target.at[h], load_sem.at[which, h]
        )

    def order(i):
        return lax.rem(first_other + i, heads)

    decay_load = pltpu.make_async_copy(decay_hbm, decay_ref, decay_sem)
    decay_load.start()

    @pl.loop(0, heads)
    def _(i):
        load(0, k_hbm, kb, order(i)).start()
        load(1, v_hbm, vb, order(i)).start()

    barrier = pltpu.get_barrier_semaphore()
    pl.semaphore_signal(barrier, inc=1, device_id={"context": mate}, device_id_type=MESH)
    for o in range(1, chips):
        there = lax.rem(chip + o, chips) * 2 + core
        pl.semaphore_signal(barrier, inc=1, device_id={"context": there}, device_id_type=MESH)
    for o in range(1, tensors):
        pl.semaphore_signal(
            barrier, inc=1, device_id={"tensor": lax.rem(rank + o, tensors)}, device_id_type=MESH
        )

    @pl.loop(0, heads)
    def _(h):
        load(2, q_hbm, qb, h).start()

    lane = lax.broadcasted_iota(jnp.int32, (heads, DIM), 1)

    def running(x):
        for shift in (1, 2, 4, 8, 16, 32, 64):
            x = x + jnp.where(lane >= shift, pltpu.roll(x, shift, 1), 0.0)
        return x

    decay_load.wait()
    before = jnp.zeros((heads, DIM), F32)
    for c in range(chunks):
        left = running(decay_ref[:, c * CHUNK : c * CHUNK + HALF])
        right = running(decay_ref[:, c * CHUNK + HALF : (c + 1) * CHUNK])
        right = right + jnp.broadcast_to(left[:, DIM - 1 :], (heads, DIM))
        total = jnp.broadcast_to(right[:, DIM - 1 :], (heads, DIM))
        cum_row[:, c * CHUNK : c * CHUNK + HALF] = left
        cum_row[:, c * CHUNK + HALF : (c + 1) * CHUNK] = right
        key_row[:, c * CHUNK : c * CHUNK + HALF] = jnp.exp(total - left)
        key_row[:, c * CHUNK + HALF : (c + 1) * CHUNK] = jnp.exp(total - right)
        chunk_decay[c] = jnp.exp(total)
        chunk_offset[c] = before
        before = before + total
    device_total[...] = before

    eye = jnp.where(
        lax.broadcasted_iota(jnp.int32, (DIM, DIM), 0) == lax.broadcasted_iota(jnp.int32, (DIM, DIM), 1), 1.0, 0.0
    ).astype(BF16)

    def device_state(h):
        load(0, k_hbm, kb, h).wait()
        load(1, v_hbm, vb, h).wait()
        held = None
        for c in range(chunks):
            rows = slice(c * CHUNK, (c + 1) * CHUNK)
            turned = dot_nt(eye, kb[h, rows, :])
            scaled = (turned * key_row[pl.ds(h, 1), rows]).astype(BF16)
            added = dot_nn(scaled, vb[h, rows, :])
            held = added if held is None else held * chunk_decay[c, pl.ds(h, 1), :] + added
            if c + 1 < chunks:
                local_in[h, c + 1] = held.astype(BF16)
        state[h, :DIM, :] = held
        state[h, DIM:, :] = jnp.broadcast_to(device_total[pl.ds(h, 1), :], (GROUP, DIM))

    def copy_a(i):
        return pltpu.make_async_remote_copy(
            src_ref=state.at[first_other + i],
            dst_ref=recv_a.at[i],
            send_sem=a_send.at[i],
            recv_sem=a_recv.at[i],
            device_id={"context": mate},
            device_id_type=MESH,
        )

    def copy_b(j):
        return pltpu.make_async_remote_copy(
            src_ref=send_b.at[j],
            dst_ref=recv_b.at[chip],
            send_sem=b_send.at[j],
            recv_sem=b_recv.at[chip],
            device_id={"context": j * 2 + core},
            device_id_type=MESH,
        )

    def arrival_b(s):
        return pltpu.make_async_remote_copy(
            src_ref=send_b.at[s],
            dst_ref=recv_b.at[s],
            send_sem=b_send.at[s],
            recv_sem=b_recv.at[s],
            device_id={"context": s * 2 + core},
            device_id_type=MESH,
        )

    def copy_c(j):
        return pltpu.make_async_remote_copy(
            src_ref=send_c.at[j],
            dst_ref=recv_c.at[chip],
            send_sem=c_send.at[j],
            recv_sem=c_recv.at[chip],
            device_id={"context": j * 2 + core},
            device_id_type=MESH,
        )

    def arrival_c(s):
        return pltpu.make_async_remote_copy(
            src_ref=send_c.at[s],
            dst_ref=recv_c.at[s],
            send_sem=c_send.at[s],
            recv_sem=c_recv.at[s],
            device_id={"context": s * 2 + core},
            device_id_type=MESH,
        )

    def copy_d(i):
        return pltpu.make_async_remote_copy(
            src_ref=send_d.at[i],
            dst_ref=entering.at[first_home + i],
            send_sem=d_send.at[i],
            recv_sem=d_recv.at[i],
            device_id={"context": mate},
            device_id_type=MESH,
        )

    def arrival_d(i):
        return pltpu.make_async_remote_copy(
            src_ref=send_d.at[i],
            dst_ref=entering.at[first_other + i],
            send_sem=d_send.at[i],
            recv_sem=d_recv.at[i],
            device_id={"context": mate},
            device_id_type=MESH,
        )

    def copy_e(half, o):
        return pltpu.make_async_remote_copy(
            src_ref=send_e.at[half],
            dst_ref=recv_e.at[half, rank],
            send_sem=e_send.at[half, o - 1],
            recv_sem=e_recv.at[half, rank],
            device_id={"tensor": lax.rem(rank + o, tensors)},
            device_id_type=MESH,
        )

    def arrival_e(half, o):
        there = lax.rem(rank + o, tensors)
        return pltpu.make_async_remote_copy(
            src_ref=send_e.at[half],
            dst_ref=recv_e.at[half, there],
            send_sem=e_send.at[half, o - 1],
            recv_sem=e_recv.at[half, there],
            device_id={"tensor": there},
            device_id_type=MESH,
        )

    part = DIM // 2
    device_state(first_other)
    pl.semaphore_wait(barrier, chips + tensors - 1)
    copy_a(0).start()

    @pl.loop(1, homes)
    def _(i):
        device_state(first_other + i)
        copy_a(i).start()

    def pair(i):
        own = state[first_home + i]
        came = recv_a[i]
        return jnp.where(core == 0, own, came), jnp.where(core == 0, came, own)

    @pl.loop(0, homes)
    def _(i):
        device_state(first_home + i)
        copy_a(i).wait_recv()
        earlier, later = pair(i)
        whole = jnp.exp(later[DIM : DIM + 1, :]) * earlier[:DIM, :] + later[:DIM, :]
        total = earlier[DIM:, :] + later[DIM:, :]
        for side in range(2):
            j = i * 2 + side
            send_b[j, :part, :] = whole[side * part : (side + 1) * part, :]
            send_b[j, part:, :] = total

            @pl.when(jnp.logical_and(j != chip, chip < chips - 1))
            def _():
                copy_b(j).start()

    lanes = lax.broadcasted_iota(jnp.int32, (GROUP, DIM), 1)

    @pl.loop(0, positions // DIM)
    def _(j):
        tile = cum_row[:, pl.ds(pl.multiple_of(j * DIM, DIM), DIM)]
        turned = jnp.concatenate([tile] * (DIM // heads), axis=0).T
        for h in range(heads):
            cum_col[h, pl.ds(pl.multiple_of(j * DIM, DIM), DIM), :] = jnp.broadcast_to(
                turned[:, h : h + 1], (DIM, DIM)
            )

    lower = lax.broadcasted_iota(jnp.int32, (DIM, DIM), 0) >= lax.broadcasted_iota(jnp.int32, (DIM, DIM), 1)

    def local(h):
        load(2, q_hbm, qb, h).wait()
        columns = pl.ds(pl.multiple_of(h * DIM, DIM), DIM)
        for c in range(chunks):
            rows = slice(c * CHUNK, (c + 1) * CHUNK)
            q, v = qb[h, rows, :], vb[h, rows, :]
            scores = dot_nt(q, kb[h, rows, :])
            at = cum_col[h, rows, :]
            by = cum_row[pl.ds(h, 1), rows]
            w00 = scores[:HALF, :HALF] * jnp.exp(jnp.where(lower, at[:HALF] - by[:, :HALF], -1e30))
            w10 = scores[HALF:, :HALF] * jnp.exp(at[HALF:] - by[:, :HALF])
            w11 = scores[HALF:, HALF:] * jnp.exp(jnp.where(lower, at[HALF:] - by[:, HALF:], -1e30))
            top = dot_nn(w00.astype(BF16), v[:HALF])
            bottom = dot_nn(jnp.concatenate([w10.astype(BF16), w11.astype(BF16)], axis=1), v)
            if c > 0:
                inter = dot_nn(q, local_in[h, c]) * jnp.exp(at)
                top = top + inter[:HALF]
                bottom = bottom + inter[HALF:]
            mixed_ref[c * CHUNK : c * CHUNK + HALF, columns] = top
            mixed_ref[c * CHUNK + HALF : (c + 1) * CHUNK, columns] = bottom

    @pl.loop(0, EARLY_HEADS)
    def _(h):
        local(h)

    prefix = jnp.zeros((part, DIM), F32)
    for s in range(chips - 1):

        @pl.when(chip == s)
        def _():
            recv_b[s] = send_b[s]

        @pl.when(chip != s)
        def _():
            arrival_b(s).wait_recv()

        prefix = prefix * jnp.exp(recv_b[s, part : part + 1, :]) + recv_b[s, :part, :]

        @pl.when(chip == s + 1)
        def _():
            recv_c[s + 1] = prefix

        @pl.when(chip != s + 1)
        def _():
            send_c[s + 1] = prefix
            copy_c(s + 1).start()

    @pl.loop(EARLY_HEADS, heads)
    def _(h):
        local(h)

    @pl.loop(0, heads)
    def _(h):
        for c in range(chunks):
            rows = slice(c * CHUNK, (c + 1) * CHUNK)
            cum_col[h, rows, :] = jnp.exp(cum_col[h, rows, :] + chunk_offset[c, pl.ds(h, 1), :])

    @pl.when(chip == 0)
    def _():
        recv_c[...] = jnp.zeros_like(recv_c)

    @pl.loop(0, homes)
    def _(i):
        for side in range(2):
            j = i * 2 + side

            @pl.when(jnp.logical_and(j != chip, chip > 0))
            def _():
                arrival_c(j).wait_recv()

        came = jnp.concatenate([recv_c[i * 2], recv_c[i * 2 + 1]], axis=0)
        earlier, _ = pair(i)
        after = jnp.exp(earlier[DIM : DIM + 1, :]) * came + earlier[:DIM, :]
        send_d[i] = jnp.where(core == 0, after, came)
        copy_d(i).start()
        entering[first_home + i] = jnp.where(core == 0, came, after)

    def head_columns(h):
        return pl.ds(pl.multiple_of(h * DIM, DIM), DIM)

    @pl.loop(0, homes)
    def _(i):
        h = first_home + i
        held = entering[h].astype(BF16)
        for c in range(chunks):
            rows = slice(c * CHUNK, (c + 1) * CHUNK)
            inter = dot_nn(qb[h, rows, :], held)
            mixed_ref[rows, head_columns(h)] = mixed_ref[rows, head_columns(h)] + cum_col[h, rows, :] * inter

    @pl.loop(0, homes)
    def _(i):
        arrival_d(i).wait_recv()

    tiles = chunks // 2
    groups = CHUNK // GROUP

    for half in range(2):

        def finish(r, found):
            c = half * tiles + r
            rows = pl.ds(pl.multiple_of(c * CHUNK, CHUNK), CHUNK)
            squares = None
            for i in range(homes):
                h = first_other + i
                inter = dot_nn(qb[h, rows, :], entering[h].astype(BF16))
                value = mixed_ref[rows, head_columns(h)] + cum_col[h, rows, :] * inter
                mixed_ref[rows, head_columns(h)] = value
                ready = mixed_ref[rows, head_columns(first_home + i)]
                both = value * value + ready * ready
                squares = both if squares is None else squares + both
            for g in range(groups):
                sums = jnp.sum(squares[g * GROUP : (g + 1) * GROUP, :], axis=1, keepdims=True)
                found = jnp.where(lanes == r * groups + g, sums, found)
            return found

        send_e[half] = lax.fori_loop(0, tiles, finish, jnp.zeros((GROUP, DIM), F32))
        for o in range(1, tensors):
            copy_e(half, o).start()

    for half in range(2):
        total = send_e[half]
        for o in range(1, tensors):
            arrival_e(half, o).wait_recv()
            total = total + recv_e[half, lax.rem(rank + o, tensors)]
        squares_ref[half] = total

    @pl.loop(0, homes)
    def _(i):
        copy_a(i).wait_send()
        copy_d(i).wait_send()

    @pl.loop(0, chips)
    def _(j):
        @pl.when(jnp.logical_and(j != chip, chip < chips - 1))
        def _():
            copy_b(j).wait_send()

        @pl.when(jnp.logical_and(j != chip, j > 0))
        def _():
            copy_c(j).wait_send()

    for half in range(2):
        for o in range(1, tensors):
            copy_e(half, o).wait_send()


def scale_kernel(mixed_ref, squares_ref, gain_ref, out_hbm, staged, sem):
    positions, width = mixed_ref.shape
    heads = width // DIM
    chunks = positions // CHUNK
    groups = CHUNK // GROUP

    def put(c):
        return pltpu.make_async_copy(staged.at[c], out_hbm.at[pl.ds(c * CHUNK, CHUNK), :], sem.at[c])

    for c in range(chunks):
        half, r = divmod(c, chunks // 2)
        scale = lax.rsqrt(squares_ref[half] / FEATURES + 1e-06)
        for g in range(0, groups, 2):
            rows = slice(c * CHUNK + g * GROUP, c * CHUNK + (g + 2) * GROUP)
            at = r * groups + g
            factor = jnp.concatenate(
                [
                    jnp.broadcast_to(scale[:, at : at + 1], (GROUP, DIM)),
                    jnp.broadcast_to(scale[:, at + 1 : at + 2], (GROUP, DIM)),
                ],
                axis=0,
            )
            for h in range(heads):
                cols = slice(h * DIM, (h + 1) * DIM)
                staged[c, g * GROUP : (g + 2) * GROUP, cols] = (
                    mixed_ref[rows, cols] * factor * gain_ref[:, cols]
                ).astype(BF16)
        put(c).start()
    for c in range(chunks):
        put(c).wait()


def shards(chips, tensors, queries, key_vectors, value_vectors, log_decay, out_gain):
    positions, width = queries.shape
    heads = width // DIM
    chunks = positions // CHUNK
    homes = heads // 2
    part = DIM // 2
    anywhere = pl.BlockSpec(memory_space=pltpu.HBM)
    vmem = pl.BlockSpec(memory_space=pltpu.VMEM)
    dma = pltpu.SemaphoreType.DMA
    mixed, squares = pl.pallas_call(
        functools.partial(attend_kernel, heads, positions, chips, tensors),
        out_shape=(
            jax.ShapeDtypeStruct((positions, width), F32),
            jax.ShapeDtypeStruct((2, GROUP, DIM), F32),
        ),
        in_specs=[anywhere] * 4,
        out_specs=(vmem, vmem),
        scratch_shapes=[
            pltpu.VMEM((heads, positions), F32),
            pltpu.VMEM((heads, positions, DIM), BF16),
            pltpu.VMEM((heads, positions, DIM), BF16),
            pltpu.VMEM((heads, positions, DIM), BF16),
            pltpu.VMEM((heads, positions), F32),
            pltpu.VMEM((heads, positions), F32),
            pltpu.VMEM((chunks, heads, DIM), F32),
            pltpu.VMEM((chunks, heads, DIM), F32),
            pltpu.VMEM((heads, DIM), F32),
            pltpu.VMEM((heads, positions, DIM), F32),
            pltpu.VMEM((heads, chunks, DIM, DIM), BF16),
            pltpu.VMEM((heads, DIM + GROUP, DIM), F32),
            pltpu.VMEM((homes, DIM + GROUP, DIM), F32),
            pltpu.VMEM((chips, part + GROUP, DIM), F32),
            pltpu.VMEM((chips, part + GROUP, DIM), F32),
            pltpu.VMEM((chips, part, DIM), F32),
            pltpu.VMEM((chips, part, DIM), F32),
            pltpu.VMEM((homes, DIM, DIM), F32),
            pltpu.VMEM((heads, DIM, DIM), F32),
            pltpu.VMEM((2, GROUP, DIM), F32),
            pltpu.VMEM((2, tensors, GROUP, DIM), F32),
            dma,
            dma((3, heads)),
            dma((homes,)),
            dma((homes,)),
            dma((chips,)),
            dma((chips,)),
            dma((chips,)),
            dma((chips,)),
            dma((homes,)),
            dma((homes,)),
            dma((2, tensors - 1)),
            dma((2, tensors)),
        ],
        compiler_params=pltpu.CompilerParams(
            collective_id=0, has_side_effects=True, vmem_limit_bytes=32 * 1024 * 1024
        ),
        name="attend",
    )(*(pltpu.with_memory_space_constraint(x, pltpu.HBM) for x in (queries, key_vectors, value_vectors, log_decay)))
    return pl.pallas_call(
        scale_kernel,
        out_shape=jax.ShapeDtypeStruct((positions, width), BF16),
        in_specs=[vmem, vmem, vmem],
        out_specs=anywhere,
        scratch_shapes=[pltpu.VMEM((chunks, CHUNK, width), BF16), dma((chunks,))],
        compiler_params=pltpu.CompilerParams(vmem_limit_bytes=16 * 1024 * 1024),
        name="scale",
    )(mixed, squares, out_gain.reshape(1, width))


def solution(mesh):
    chips, tensors = mesh.shape["context"] // 2, mesh.shape["tensor"]
    placed = (
        P(("dp", "context"), "tensor"),
        P(("dp", "context"), "tensor"),
        P(("dp", "context"), "tensor"),
        P("tensor", ("dp", "context")),
        P("tensor"),
    )
    return jax.shard_map(
        functools.partial(shards, chips, tensors),
        mesh=mesh,
        in_specs=placed,
        out_specs=P(("dp", "context"), "tensor"),
        check_vma=False,
    )
```
